32 devices in a mesh: seq: 16 (over z, y, core), head: 2 (over x).
Axes of the slice: x: 2, y: 2, z: 4, core: 2. Of those that a mesh axis runs over, the one named last changes fastest.
Arguments:
- queries: bfloat16 [8192, 2048], P('seq', 'head'), may hold values from -200 to 200
- key_heads: bfloat16 [8192, 1024], P('seq', 'head'), may hold values from -8 to 8
- value_heads: bfloat16 [8192, 1024], P('seq', 'head'), may hold values from -6 to 6
- lengths: int32 [16], replicated, may hold values from 1 to 2048, 8192 in all
- gate_inputs: bfloat16 [2, 8192, 2048], P(None, 'seq', 'head'), may hold values from -6 to 6
- cotangent: bfloat16 [8192, 2560], P('seq', 'head'), may hold values from -6 to 6
- out_weight: bfloat16 [2, 2048, 2560], P(None, 'head'), may hold values from -0.125 to 0.125
- adapter_down: bfloat16 [2, 2048, 64], P(None, 'head'), may hold values from -0.125 to 0.125
- adapter_up: bfloat16 [2, 64, 2560], replicated, may hold values from -0.125 to 0.125
Outputs:
- query_gradient: bfloat16 [8192, 2048], P('seq', 'head')
- key_gradient: bfloat16 [8192, 1024], P('seq', 'head')
- value_gradient: bfloat16 [8192, 1024], P('seq', 'head')
- gate_gradient: bfloat16 [2, 8192, 2048], P(None, 'seq', 'head')
- down_gradient: float32 [2, 2048, 64], P(None, 'head')
- up_gradient: float32 [2, 64, 2560], P(None, None, 'head')
The draws below stay inside these ranges and needn't reach their ends.
Inputs may be any that keep to these rules, and one draw needn't show every extreme that they name: The lengths sum to 8192.
All inputs are finite; a program needn't handle non-finite values.
Results may differ from the reference program's by a relative error of at most 0.0075.
Values may be sent and summed in bfloat16 or wider, within the bound.
No kernel may reach another device: no remote copies, remote signals or barrier semaphores. Data moves between devices by JAX's collectives and lax.ppermute only.
A program may use at most 128 MiB of HBM per device.

```python
import math
import jax
import jax.numpy as jnp
import numpy as np
from jax import lax

D = 2560
HEAD_DIM = 64
QHEADS = 32
KVHEADS = 16
RANK = 64
WIN = 512
DOCS = 16
TOK_DEV = 512
SEQ = 8192
QW = 2048
KW = 1024
DOCMOST = 2048


def paired_rows(key):
    query_key = jax.random.fold_in(key, 101)
    keys_key = jax.random.fold_in(key, 102)
    query_all = jax.random.normal(query_key, (SEQ, QHEADS * HEAD_DIM), jnp.float32)
    keys_all = jax.random.normal(keys_key, (SEQ, KVHEADS * HEAD_DIM), jnp.float32)
    return (jnp.clip(query_all, -200.0, 200.0), jnp.clip(keys_all, -8.0, 8.0))


def draw_queries(key, part):
    return paired_rows(key)[0].astype(jnp.bfloat16)


def draw_key_heads(key, part):
    return paired_rows(key)[1].astype(jnp.bfloat16)


def levels(rng, dims, split, least, top_value):
    level = 1.0
    for position, blocks in split:
        heights = jax.random.uniform(jax.random.fold_in(jax.random.fold_in(rng, 6), position), (blocks,), jnp.float32, least / len(split), top_value / len(split))
        level = level * jnp.repeat(jnp.exp(heights), dims[position] // blocks).reshape((-1,) + (1,) * (len(dims) - 1 - position))
    return level


def length_profile(count, total, bound, lean):
    portions = [(1 << 20) // math.isqrt(grade ** lean) + 1 for grade in range(2, count + 1)]
    surplus, counts = total - bound - (count - 1), [1] * (count - 1)
    while surplus > 0:
        free = [i for i in range(count - 1) if counts[i] < bound]
        pool, remaining = sum([portions[i] for i in free]), surplus
        for i in free:
            addition = min(bound - counts[i], max(1, remaining * portions[i] // pool), surplus)
            counts[i] = counts[i] + addition
            surplus = surplus - addition
    return np.array([bound] + counts)


def uneven(rng, number_of, total, most, lean):
    if number_of == 2:
        one = jax.random.randint(rng, (), max(1, total - most), min(most, total - 1) + 1)
        return jnp.stack([one, total - one])
    sizes = jnp.asarray(length_profile(number_of, total, most, lean), jnp.int32)
    pairs = (number_of - 1) // 2
    donor, sink = sizes[1:1 + 2 * pairs:2], sizes[2:2 + 2 * pairs:2]
    margin = jnp.minimum(donor - 1, most - sink)
    passed = jax.random.randint(jax.random.fold_in(rng, 1), (pairs,), 0, 1 << 20) % (margin + 1)
    sizes = sizes.at[1:1 + 2 * pairs:2].set(donor - passed).at[2:2 + 2 * pairs:2].set(sink + passed)
    return sizes[jax.random.permutation(jax.random.fold_in(rng, 2), number_of)]


def centred(key, extent, deviation, bound, shards=(), kind=jnp.bfloat16):
    entries = jax.random.normal(key, extent, jnp.float32) * deviation
    if len(shards) > 0:
        entries = levels(key, extent, shards, -0.22, 0.18) * entries
    return jnp.clip(entries, min=-bound, max=bound).astype(kind)


def setup_inputs(seed: int = 0) -> dict:
    arg_keys = jax.random.split(jax.random.key(seed), 10)
    queries = draw_queries(jax.random.fold_in(arg_keys[9], 71), 0)
    key_heads = draw_key_heads(jax.random.fold_in(arg_keys[9], 71), 0)
    value_heads = centred(arg_keys[2], (SEQ, KW), 1.0, 6.0, ((0, 16), (1, 2)))
    lengths = uneven(arg_keys[3], DOCS, SEQ, DOCMOST, 2).astype(jnp.int32)
    gate_inputs = centred(arg_keys[4], (2, SEQ, QW), 1.0, 6.0, ((1, 16), (2, 2)))
    cotangent = centred(arg_keys[5], (SEQ, D), 1.0, 6.0, ((0, 16), (1, 2)))
    out_weight = centred(arg_keys[6], (2, QW, D), QW ** -0.5, 0.125, ((1, 2),))
    adapter_down = centred(arg_keys[7], (2, QW, RANK), QW ** -0.5, 0.125, ((1, 2),))
    adapter_up = centred(arg_keys[8], (2, RANK, D), D ** -0.5, 0.125)
    return dict(queries=queries, key_heads=key_heads, value_heads=value_heads, lengths=lengths, gate_inputs=gate_inputs, cotangent=cotangent, out_weight=out_weight, adapter_down=adapter_down, adapter_up=adapter_up)


masked_score = -1.0e30


def rounded(matrix):
    return lax.optimization_barrier(matrix.astype(jnp.bfloat16)).astype(jnp.float32)


def segment_of(lengths, positions):
    ends = jnp.cumsum(lengths)
    return jnp.sum((ends[None, :] <= positions[:, None]).astype(jnp.int32), axis=1)


def silu_slope(inputs):
    sigma = jax.nn.sigmoid(inputs)
    return sigma * (1.0 + inputs * (1.0 - sigma))


def block_mask(query_pos, key_pos, query_seg, key_seg):
    offset = query_pos[:, None] - key_pos[None, :]
    return (offset >= 0) & (offset < WIN) & (key_pos[None, :] >= 0) & (query_seg[:, None] == key_seg[None, :])


def block_probs(query_block, key_block, allowed):
    groups = QHEADS // KVHEADS
    query_matrix = query_block.astype(jnp.float32).reshape(query_block.shape[0], KVHEADS, groups, HEAD_DIM)
    key_matrix = key_block.astype(jnp.float32).reshape(key_block.shape[0], KVHEADS, HEAD_DIM)
    scores = jnp.einsum("qhge,khe->hgqk", query_matrix, key_matrix) * (HEAD_DIM ** -0.5)
    scores = jnp.where(allowed[None, None], scores, masked_score)
    highest = jnp.max(scores, axis=-1, keepdims=True)
    weights = jnp.exp(scores - highest)
    return weights / jnp.sum(weights, axis=-1, keepdims=True)


def reference(queries, key_heads, value_heads, lengths, gate_inputs, cotangent, out_weight, adapter_down, adapter_up):
    total_rows = queries.shape[0]
    block_rows = min(512, TOK_DEV)
    key_span = block_rows + WIN
    groups = QHEADS // KVHEADS
    block_count = total_rows // block_rows
    positions = jnp.arange(total_rows + WIN, dtype=jnp.int32) - WIN
    segments = segment_of(lengths, positions)
    padding = jnp.zeros((WIN, KVHEADS * HEAD_DIM), jnp.bfloat16)
    keys_ext = jnp.concatenate([padding, key_heads], axis=0)
    values_ext = jnp.concatenate([padding, value_heads], axis=0)

    def window(first_row):
        query_block = lax.dynamic_slice_in_dim(queries, first_row, block_rows, 0)
        key_block = lax.dynamic_slice_in_dim(keys_ext, first_row, key_span, 0)
        value_block = lax.dynamic_slice_in_dim(values_ext, first_row, key_span, 0)
        allowed = block_mask(lax.dynamic_slice_in_dim(positions, first_row + WIN, block_rows, 0),
                             lax.dynamic_slice_in_dim(positions, first_row, key_span, 0),
                             lax.dynamic_slice_in_dim(segments, first_row + WIN, block_rows, 0),
                             lax.dynamic_slice_in_dim(segments, first_row, key_span, 0))
        return query_block, key_block, value_block, allowed

    def forward_block(state_carry, number):
        first_row = (number * block_rows).astype(jnp.int32)
        query_block, key_block, value_block, allowed = window(first_row)
        weights = block_probs(query_block, key_block, allowed)
        value_matrix = value_block.astype(jnp.float32).reshape(key_span, KVHEADS, HEAD_DIM)
        output = jnp.einsum("hgqk,khe->qhge", rounded(weights), value_matrix)
        return state_carry, output.reshape(block_rows, QHEADS * HEAD_DIM)

    numbers = jnp.arange(block_count, dtype=jnp.int32)
    _, outputs = lax.scan(forward_block, jnp.zeros((), jnp.float32), numbers)
    attended = outputs.reshape(total_rows, QHEADS * HEAD_DIM)
    memory = rounded(attended)
    scale_sum = total_rows ** -0.5
    memory_grad = jnp.zeros(attended.shape, jnp.float32)
    gate_parts = []
    down_parts = []
    up_parts = []
    for section in range(2):
        gate_raw = gate_inputs[section].astype(jnp.float32)
        activation = jax.nn.silu(gate_raw)
        hidden = (memory * activation).astype(jnp.bfloat16)
        back_proj = jnp.dot(cotangent, adapter_up[section].T, preferred_element_type=jnp.float32).astype(jnp.bfloat16)
        fore_proj = jnp.dot(hidden, adapter_down[section], preferred_element_type=jnp.float32).astype(jnp.bfloat16)
        hidden_grad = jnp.dot(cotangent, out_weight[section].T, preferred_element_type=jnp.float32)
        hidden_grad = hidden_grad + jnp.dot(back_proj, adapter_down[section].T, preferred_element_type=jnp.float32)
        down_parts.append(jnp.dot(hidden.T, back_proj, preferred_element_type=jnp.float32) * scale_sum)
        up_parts.append(jnp.dot(fore_proj.T, cotangent, preferred_element_type=jnp.float32) * scale_sum)
        gate_parts.append((hidden_grad * memory * silu_slope(gate_raw)).astype(jnp.bfloat16))
        memory_grad = memory_grad + hidden_grad * activation
    memory_grad = memory_grad.astype(jnp.bfloat16)

    def backward_block(state_carry, number):
        key_grad, value_grad = state_carry
        first_row = (number * block_rows).astype(jnp.int32)
        query_block, key_block, value_block, allowed = window(first_row)
        weights = block_probs(query_block, key_block, allowed)
        out_block = lax.dynamic_slice_in_dim(memory_grad, first_row, block_rows, 0).astype(jnp.float32)
        out_block = out_block.reshape(block_rows, KVHEADS, groups, HEAD_DIM)
        attended_block = lax.dynamic_slice_in_dim(attended, first_row, block_rows, 0).reshape(block_rows, KVHEADS, groups, HEAD_DIM)
        value_matrix = value_block.astype(jnp.float32).reshape(key_span, KVHEADS, HEAD_DIM)
        key_matrix = key_block.astype(jnp.float32).reshape(key_span, KVHEADS, HEAD_DIM)
        query_matrix = query_block.astype(jnp.float32).reshape(block_rows, KVHEADS, groups, HEAD_DIM)
        value_part = jnp.einsum("hgqk,qhge->khe", rounded(weights), out_block).reshape(key_span, -1)
        weight_grad = jnp.einsum("qhge,khe->hgqk", out_block, value_matrix)
        row_delta = jnp.transpose(jnp.sum(out_block * attended_block, axis=-1), (1, 2, 0))[..., None]
        score_grad = rounded(weights * (weight_grad - row_delta) * (HEAD_DIM ** -0.5))
        query_part = jnp.einsum("hgqk,khe->qhge", score_grad, key_matrix).reshape(block_rows, -1)
        key_part = jnp.einsum("hgqk,qhge->khe", score_grad, query_matrix).reshape(key_span, -1)
        key_grad = lax.dynamic_update_slice_in_dim(
            key_grad, lax.dynamic_slice_in_dim(key_grad, first_row, key_span, 0) + key_part, first_row, 0)
        value_grad = lax.dynamic_update_slice_in_dim(
            value_grad, lax.dynamic_slice_in_dim(value_grad, first_row, key_span, 0) + value_part, first_row, 0)
        return (key_grad, value_grad), query_part.astype(jnp.bfloat16)

    zero_ext = jnp.zeros((total_rows + WIN, KVHEADS * HEAD_DIM), jnp.float32)
    (key_grad, value_grad), query_parts = lax.scan(backward_block, (zero_ext, zero_ext), numbers)
    query_gradient = query_parts.reshape(total_rows, QHEADS * HEAD_DIM)
    key_gradient = key_grad[WIN:].astype(jnp.bfloat16)
    value_gradient = value_grad[WIN:].astype(jnp.bfloat16)
    return (query_gradient, key_gradient, value_gradient, jnp.stack(gate_parts),
            jnp.stack(down_parts), jnp.stack(up_parts))
```

```python
import functools
import math

import jax
import jax.numpy as jnp
from jax import lax
from jax.experimental import pallas as pl
from jax.experimental.pallas import tpu as pltpu
from jax.sharding import PartitionSpec as P

HEAD_DIM = 64
WIN = 512
RANK = 64
CHUNK = 256
BLOCK = 256
SPAN = CHUNK + WIN

masked_score = -1e30

NT = (((1,), (1,)), ((), ()))
f32 = jnp.float32
bf16 = jnp.bfloat16


def shifted(value, axis, steps):
    count = lax.axis_size(axis)
    first, last = (max(0, -steps), min(count, count - steps))
    return lax.ppermute(value, axis, [(source, source + steps) for source in range(first, last)])


def swapped(value, axis, bit):
    count = lax.axis_size(axis)
    return lax.ppermute(value, axis, [(source, source ^ bit) for source in range(count)])


def total_over(value, axis):
    count = lax.axis_size(axis)
    index = lax.axis_index(axis)
    bits = [1 << place for place in range(count.bit_length() - 1)]
    for bit in bits:
        half = value.shape[0] // 2
        side = (index // bit) % 2
        keep = lax.dynamic_slice_in_dim(value, side * half, half, 0)
        send = lax.dynamic_slice_in_dim(value, (1 - side) * half, half, 0)
        value = keep + swapped(send.astype(bf16), axis, bit).astype(f32)
    value = value.astype(bf16)
    for bit in reversed(bits):
        side = (index // bit) % 2
        other = swapped(value, axis, bit)
        value = jnp.where(
            side == 0,
            jnp.concatenate([value, other], axis=0),
            jnp.concatenate([other, value], axis=0),
        )
    return value


def dot(left, right, dims=(((1,), (0,)), ((), ()))):
    return lax.dot_general(left, right, dims, preferred_element_type=f32)


def forward_kernel(
    docs,
    chunks,
    meta,
    q_ref,
    k_ref,
    v_ref,
    hk_ref,
    hv_ref,
    gate_ref,
    down_ref,
    back_ref,
    p_ref,
    ot_ref,
    mem_ref,
    vext_ref,
    ktext_ref,
    fore_ref,
    down_out_ref,
    bias_ref,
):
    @pl.when(pl.program_id(0) == 0)
    def _():
        anchor = meta[0]
        for chunk in range(chunks):
            place = anchor + chunk * CHUNK + lax.broadcasted_iota(jnp.int32, (1, CHUNK), 1)
            low = jnp.maximum(place - (WIN - 1), 0)
            end = jnp.int32(0)
            for doc in range(docs):
                end = end + meta[1 + doc]
                low = jnp.maximum(low, jnp.where(place >= end, end, 0))
            low = low - (anchor - WIN + chunk * CHUNK)
            row = lax.broadcasted_iota(jnp.int32, (SPAN, CHUNK), 0)
            col = lax.broadcasted_iota(jnp.int32, (SPAN, CHUNK), 1)
            seen = (row >= low) & (row <= col + WIN)
            bias_ref[chunk] = jnp.where(seen, 0.0, masked_score)
        fore_ref[...] = jnp.zeros_like(fore_ref)

    slope = HEAD_DIM ** (-0.5) * math.log2(math.e)
    keys = jnp.concatenate([hk_ref[...], k_ref[...]], axis=0)
    values = jnp.concatenate([hv_ref[...], v_ref[...]], axis=0)
    vext_ref[...] = values
    ktext_ref[...] = keys.T
    values_t = values.T
    for chunk in range(chunks):
        rows = slice(chunk * CHUNK, (chunk + 1) * CHUNK)
        span = slice(chunk * CHUNK, chunk * CHUNK + SPAN)
        for head in range(BLOCK // HEAD_DIM):
            pair = head // 2
            key = keys[span, pair * HEAD_DIM : (pair + 1) * HEAD_DIM]
            query = q_ref[rows, head * HEAD_DIM : (head + 1) * HEAD_DIM]
            scores = dot(key, query, NT) + bias_ref[chunk]
            highest = jnp.max(scores, axis=0, keepdims=True)
            weights = jnp.exp2((scores - highest) * slope)
            whole = jnp.sum(weights, axis=0, keepdims=True)
            low_weights = (weights * (1.0 / whole)).astype(bf16)
            p_ref[head, chunk] = low_weights
            value_t = values_t[pair * HEAD_DIM : (pair + 1) * HEAD_DIM, span]
            ot_ref[head * HEAD_DIM : (head + 1) * HEAD_DIM, rows] = dot(value_t, low_weights)
    memory = ot_ref[...].T.astype(bf16)
    mem_ref[...] = memory
    memory = memory.astype(f32)
    for section in range(2):
        raw = gate_ref[section].astype(f32)
        hidden = (memory * (raw * jax.nn.sigmoid(raw))).astype(bf16)
        part = slice(section * RANK, (section + 1) * RANK)
        fore_ref[:, part] += dot(hidden, down_ref[:, part])
        down_out_ref[part, :] = dot(back_ref[part, :], hidden)


def forward_call(meta, queries, key_heads, value_heads, halo, gates, down_cat, back_t):
    rows, width = queries.shape
    kv_width = key_heads.shape[1]
    chunks = rows // CHUNK
    blocks = width // BLOCK
    docs = meta.shape[0] - 1
    kv_block = BLOCK // 2
    ext = rows + WIN
    heads = width // HEAD_DIM
    col = lambda j, m: (0, j)
    halo_blocks = kv_width // kv_block
    grid_spec = pltpu.PrefetchScalarGridSpec(
        num_scalar_prefetch=1,
        grid=(blocks,),
        in_specs=[
            pl.BlockSpec((rows, BLOCK), col),
            pl.BlockSpec((rows, kv_block), col),
            pl.BlockSpec((rows, kv_block), col),
            pl.BlockSpec((WIN, kv_block), col),
            pl.BlockSpec((WIN, kv_block), col),
            pl.BlockSpec((2, rows, BLOCK), lambda j, m: (0, 0, j)),
            pl.BlockSpec((BLOCK, 2 * RANK), lambda j, m: (j, 0)),
            pl.BlockSpec((2 * RANK, rows), lambda j, m: (0, 0)),
        ],
        out_specs=[
            pl.BlockSpec((BLOCK // HEAD_DIM, chunks, SPAN, CHUNK), lambda j, m: (j, 0, 0, 0)),
            pl.BlockSpec((BLOCK, rows), lambda j, m: (j, 0)),
            pl.BlockSpec((rows, BLOCK), col),
            pl.BlockSpec((ext, kv_block), col),
            pl.BlockSpec((kv_block, ext), lambda j, m: (j, 0)),
            pl.BlockSpec((rows, 2 * RANK), lambda j, m: (0, 0)),
            pl.BlockSpec((2 * RANK, BLOCK), col),
        ],
        scratch_shapes=[pltpu.VMEM((chunks, SPAN, CHUNK), f32)],
    )
    return pl.pallas_call(
        functools.partial(forward_kernel, docs, chunks),
        grid_spec=grid_spec,
        out_shape=[
            jax.ShapeDtypeStruct((heads, chunks, SPAN, CHUNK), bf16),
            jax.ShapeDtypeStruct((width, rows), f32),
            jax.ShapeDtypeStruct((rows, width), bf16),
            jax.ShapeDtypeStruct((ext, kv_width), bf16),
            jax.ShapeDtypeStruct((kv_width, ext), bf16),
            jax.ShapeDtypeStruct((rows, 2 * RANK), f32),
            jax.ShapeDtypeStruct((2 * RANK, width), f32),
        ],
        compiler_params=pltpu.CompilerParams(dimension_semantics=("arbitrary",)),
        cost_estimate=pl.CostEstimate(
            flops=4 * heads * chunks * SPAN * CHUNK * HEAD_DIM,
            bytes_accessed=heads * chunks * SPAN * CHUNK * 2 + 10 * rows * width,
            transcendentals=heads * chunks * SPAN * CHUNK,
        ),
        name="window_forward",
    )(meta, queries, key_heads, value_heads, halo[0], halo[1], gates, down_cat, back_t)


def backward_kernel(chunk, pieces, carried, meta, *refs):
    cots, refs = refs[:pieces], refs[pieces:]
    weights, refs = refs[:pieces], refs[pieces:]
    (back_ref, down_ref, gate_ref, mem_ref, p_ref, ot_ref, vext_ref, ktext_ref, q_ref), refs = (
        refs[:9],
        refs[9:],
    )
    if carried:
        carry_ref, refs = refs[0], refs[3:]
    gate_out_ref, dq_ref, final_ref, rest_ref = refs

    memory = mem_ref[...].astype(f32)
    memory_grad = None
    for section in range(2):
        part = slice(section * RANK, (section + 1) * RANK)
        hidden_grad = dot(back_ref[:, part], down_ref[:, part], NT)
        for piece in range(pieces):
            hidden_grad += dot(cots[piece][...], weights[piece][section], NT)
        raw = gate_ref[section].astype(f32)
        sigma = jax.nn.sigmoid(raw)
        gate_out_ref[section] = (
            hidden_grad * memory * (sigma * (1.0 + raw * (1.0 - sigma)))
        ).astype(bf16)
        term = hidden_grad * (raw * sigma)
        memory_grad = term if memory_grad is None else memory_grad + term
    out_grad = memory_grad.astype(bf16)
    out_grad_t = out_grad.T
    span = slice(chunk * CHUNK, chunk * CHUNK + SPAN)
    dqs, dks, dvs = [], [], []
    for pair in range(BLOCK // HEAD_DIM // 2):
        lanes = slice(pair * HEAD_DIM, (pair + 1) * HEAD_DIM)
        value = vext_ref[span, lanes]
        key_t = ktext_ref[lanes, span]
        dk = dv = None
        for group in range(2):
            head = 2 * pair + group
            own = slice(head * HEAD_DIM, (head + 1) * HEAD_DIM)
            grad_t = out_grad_t[own, :]
            row_delta = jnp.sum(grad_t.astype(f32) * ot_ref[own, :], axis=0, keepdims=True)
            probs = p_ref[head, 0]
            probs_grad = dot(value, grad_t)
            score_grad = (probs.astype(f32) * (probs_grad - row_delta)).astype(bf16)
            dqs.append(dot(key_t, score_grad))
            dk_part = dot(score_grad, q_ref[:, own])
            dv_part = dot(probs, out_grad[:, own])
            dk = dk_part if dk is None else dk + dk_part
            dv = dv_part if dv is None else dv + dv_part
        dks.append(dk)
        dvs.append(dv)
    scale = HEAD_DIM ** (-0.5)
    dq_ref[...] = (jnp.concatenate(dqs, axis=0) * scale).T.astype(bf16)
    for which, total in enumerate(
        (jnp.concatenate(dks, axis=1) * scale, jnp.concatenate(dvs, axis=1))
    ):
        first, rest = total[:CHUNK], total[CHUNK:]
        if carried:
            first = first + carry_ref[which, :CHUNK]
            rest = jnp.concatenate(
                [rest[: WIN - CHUNK] + carry_ref[which, CHUNK:], rest[WIN - CHUNK :]], axis=0
            )
        final_ref[which] = first.astype(bf16)
        rest_ref[which] = rest


def backward_call(
    meta, chunk, cots, out_weight, back, down_cat, gates, memory, state, queries, carry, filled
):
    probs, attended_t, vext, ktext = state
    rows, width = queries.shape
    kv_width = vext.shape[1]
    kv_block = BLOCK // 2
    ext = rows + WIN
    blocks = width // BLOCK
    pieces = len(cots)
    feats = cots[0].shape[1]
    here = lambda j, m: (chunk, j)
    in_specs = [pl.BlockSpec((CHUNK, feats), lambda j, m: (0, 0)) for _ in cots]
    for piece in range(pieces):
        in_specs.append(
            pl.BlockSpec((2, BLOCK, feats), lambda j, m, piece=piece: (0, j, m[1 + piece]))
        )
    in_specs += [
        pl.BlockSpec((CHUNK, 2 * RANK), lambda j, m: (chunk, 0)),
        pl.BlockSpec((BLOCK, 2 * RANK), lambda j, m: (j, 0)),
        pl.BlockSpec((2, CHUNK, BLOCK), lambda j, m: (0, chunk, j)),
        pl.BlockSpec((CHUNK, BLOCK), here),
        pl.BlockSpec((BLOCK // HEAD_DIM, 1, SPAN, CHUNK), lambda j, m: (j, chunk, 0, 0)),
        pl.BlockSpec((BLOCK, CHUNK), lambda j, m: (j, chunk)),
        pl.BlockSpec((ext, kv_block), lambda j, m: (0, j)),
        pl.BlockSpec((kv_block, ext), lambda j, m: (j, 0)),
        pl.BlockSpec((CHUNK, BLOCK), here),
    ]
    operands = [meta, *cots, *([out_weight] * pieces), back, down_cat, gates, memory]
    operands += [probs, attended_t, vext, ktext, queries]
    aliases = {}
    if carry is not None:
        in_specs.append(pl.BlockSpec((2, WIN, kv_block), lambda j, m: (0, 0, j)))
        in_specs += [pl.BlockSpec(memory_space=pl.ANY)] * 2
        operands += [carry, *filled]
        aliases = {len(operands) - 2: 0, len(operands) - 1: 1}
    grid_spec = pltpu.PrefetchScalarGridSpec(
        num_scalar_prefetch=1,
        grid=(blocks,),
        in_specs=in_specs,
        out_specs=[
            pl.BlockSpec((2, CHUNK, BLOCK), lambda j, m: (0, chunk, j)),
            pl.BlockSpec((CHUNK, BLOCK), here),
            pl.BlockSpec((2, CHUNK, kv_block), lambda j, m: (0, 0, j)),
            pl.BlockSpec((2, WIN, kv_block), lambda j, m: (0, 0, j)),
        ],
    )
    heads = width // HEAD_DIM
    return pl.pallas_call(
        functools.partial(backward_kernel, chunk, pieces, carry is not None),
        grid_spec=grid_spec,
        out_shape=[
            jax.ShapeDtypeStruct((2, rows, width), bf16),
            jax.ShapeDtypeStruct((rows, width), bf16),
            jax.ShapeDtypeStruct((2, CHUNK, kv_width), bf16),
            jax.ShapeDtypeStruct((2, WIN, kv_width), f32),
        ],
        input_output_aliases=aliases,
        compiler_params=pltpu.CompilerParams(dimension_semantics=("arbitrary",)),
        cost_estimate=pl.CostEstimate(
            flops=8 * heads * SPAN * CHUNK * HEAD_DIM + 4 * CHUNK * width * feats * pieces,
            bytes_accessed=2 * heads * SPAN * CHUNK + 4 * width * feats * pieces,
            transcendentals=2 * CHUNK * width,
        ),
        name="window_backward",
    )(*operands)


def per_device(
    queries,
    key_heads,
    value_heads,
    lengths,
    gate_inputs,
    cotangent,
    out_weight,
    adapter_down,
    adapter_up,
):
    rows, width = queries.shape
    feats = cotangent.shape[1]
    seq_count = lax.axis_size("seq")
    head_count = lax.axis_size("head")
    head_index = lax.axis_index("head")
    chunks = rows // CHUNK

    halo = shifted((key_heads, value_heads), "seq", 1)
    up_cat = adapter_up.reshape(2 * RANK, -1)
    up_own = lax.dynamic_slice_in_dim(up_cat, head_index * feats, feats, 1)
    back_part = dot(cotangent, up_own, NT)
    paired = head_count == 2 and feats % 128 == 0
    if paired:
        back_sum = back_part + swapped(back_part.astype(bf16), "head", 1).astype(f32)
        cots = [
            (
                cotangent[chunk * CHUNK : (chunk + 1) * CHUNK],
                swapped(cotangent[chunk * CHUNK : (chunk + 1) * CHUNK], "head", 1),
            )
            for chunk in range(chunks)
        ]
        columns = jnp.stack([head_index, 1 - head_index]).astype(jnp.int32)
    else:
        back_sum = lax.psum(back_part, "head")
        full = lax.all_gather(cotangent, "head", axis=1, tiled=True)
        cots = [(full[chunk * CHUNK : (chunk + 1) * CHUNK],) for chunk in range(chunks)]
        columns = jnp.zeros((1,), jnp.int32)
    back = back_sum.astype(bf16)
    down_cat = jnp.concatenate([adapter_down[0], adapter_down[1]], axis=1)
    anchor = (lax.axis_index("seq") * rows).astype(jnp.int32)
    meta = jnp.concatenate([anchor[None], lengths.astype(jnp.int32)])

    probs, attended_t, memory, vext, ktext, fore_part, down_part = forward_call(
        meta, queries, key_heads, value_heads, halo, gate_inputs, down_cat, back.T
    )
    if paired:
        fore_sum = fore_part + swapped(fore_part.astype(bf16), "head", 1).astype(f32)
    else:
        fore_sum = lax.psum(fore_part, "head")
    up_part = dot(fore_sum.astype(bf16), cotangent, (((0,), (0,)), ((), ())))
    total = total_over(jnp.concatenate([down_part, up_part], axis=1), "seq")
    total = total.astype(f32) * (rows * seq_count) ** (-0.5)
    down_gradient = jnp.transpose(total[:, :width].reshape(2, RANK, width), (0, 2, 1))
    up_gradient = total[:, width:].reshape(2, RANK, feats)

    state = (probs, attended_t, vext, ktext)
    back_meta = jnp.concatenate([jnp.zeros((1,), jnp.int32), columns])
    carry, filled, returned = None, None, []
    for chunk in range(chunks):
        gate_gradient, query_gradient, final, carry = backward_call(
            back_meta,
            chunk,
            cots[chunk],
            out_weight,
            back,
            down_cat,
            gate_inputs,
            memory,
            state,
            queries,
            carry,
            filled,
        )
        filled = (gate_gradient, query_gradient)
        returned.append(shifted(final, "seq", -1))
    own = (carry + jnp.concatenate(returned, axis=1).astype(f32)).astype(bf16)
    return (query_gradient, own[0], own[1], gate_gradient, down_gradient, up_gradient)


def solution(mesh):
    in_specs = (
        P("seq", "head"),
        P("seq", "head"),
        P("seq", "head"),
        P(),
        P(None, "seq", "head"),
        P("seq", "head"),
        P(None, "head", None),
        P(None, "head", None),
        P(),
    )
    out_specs = (
        P("seq", "head"),
        P("seq", "head"),
        P("seq", "head"),
        P(None, "seq", "head"),
        P(None, "head", None),
        P(None, None, "head"),
    )
    return jax.shard_map(
        per_device, mesh=mesh, in_specs=in_specs, out_specs=out_specs, check_vma=False
    )
```
